32 devices in a mesh: row: 4 (over x, core), col: 8 (over z, y).
Axes of the slice: x: 2, y: 2, z: 4, core: 2. Of those that a mesh axis runs over, the one named last changes fastest.
Arguments:
- tokens: bfloat16 [128, 12288], P('col', 'row'), may hold values from -6 to 6
- w_in: bfloat16 [12288, 24576], P('row', 'col'), may hold values from -0.078125 to 0.078125
- w_out: bfloat16 [24576, 12288], P('col', 'row'), may hold values from -0.0546875 to 0.0546875
- mask_in: int32 [96, 192], P('row', 'col'), may hold values 0 or 1
- mask_out: int32 [192, 96], P('col', 'row'), may hold values 0 or 1
- out_grad: bfloat16 [128, 12288], P('col', 'row'), may hold values from -1.5 to 1.5
Outputs:
- mixed: bfloat16 [128, 12288], P('col', 'row')
- tokens_grad: bfloat16 [128, 12288], P('col', 'row')
- w_in_grad: bfloat16 [12288, 24576], P('row', 'col')
- w_out_grad: bfloat16 [24576, 12288], P('col', 'row')
The draws below stay inside these ranges and needn't reach their ends.
Inputs may be any that keep to these rules, and one draw needn't show every extreme that they name: `mask_in`: one flag per block. `mask_out`: one flag per block.
All inputs are finite; a program needn't handle non-finite values.
Results may differ from the reference program's by a relative error of at most 0.0049.
Values may be sent and summed in bfloat16 or wider, within the bound.
A program may use at most 192 MiB of HBM per device.

```python
import jax
import jax.numpy as jnp

D = 12288
FF = 24576
BLK = 128
TOKENS = 128


def set_ends(entries, own_key, least, high):
    longest = entries.shape.index(max(entries.shape))
    spots = []
    for shift in (0, 1):
        where = [jax.random.randint(jax.random.fold_in(own_key, axis), (), 0, length) for axis, length in enumerate(entries.shape)]
        where[longest] = (where[longest] + shift) % entries.shape[longest]
        spots.append(tuple(where))
    return entries.at[spots[0]].set(least).at[spots[1]].set(high)


def steps_of(own_key, shape, shards, least, top_value):
    factor_of, own = 1.0, jax.random.fold_in(own_key, 6)
    for dim, parts in shards:
        steps = jnp.exp(jax.random.uniform(jax.random.fold_in(own, dim), (parts,), jnp.float32, least / len(shards), top_value / len(shards)))
        factor_of = factor_of * jnp.repeat(steps, shape[dim] // parts).reshape([-1 if axis == dim else 1 for axis in range(len(shape))])
    return factor_of


def centred(key, extent, spread, reach, pieces=(), held_as=jnp.bfloat16):
    drawn = jax.random.normal(key, extent, jnp.float32) * spread
    if len(pieces) > 0:
        drawn = steps_of(key, extent, pieces, -0.22, 0.18) * drawn
    return jnp.clip(drawn, min=-reach, max=reach).astype(held_as)


def setup_inputs(seed: int = 0) -> dict:
    seeds = jax.random.split(jax.random.key(seed), 7)
    return {
        "tokens": centred(seeds[0], (TOKENS, D), 1.0, 6.0, ((0, 8), (1, 4))),
        "w_in": centred(seeds[1], (D, FF), (D // 2) ** -0.5, 0.078125, ((0, 4), (1, 8))),
        "w_out": centred(seeds[2], (FF, D), (FF // 2) ** -0.5, 0.0546875, ((0, 8), (1, 4))),
        "mask_in": set_ends((jax.random.randint(seeds[3], (D // BLK, FF // BLK), 0, 2) < 1).astype(jnp.int32), jax.random.fold_in(seeds[3], 1), 0, 1),
        "mask_out": set_ends((jax.random.randint(seeds[4], (FF // BLK, D // BLK), 0, 2) < 1).astype(jnp.int32), jax.random.fold_in(seeds[4], 1), 0, 1),
        "out_grad": centred(seeds[5], (TOKENS, D), 0.25, 1.5, ((0, 8), (1, 4))),
    }


def apply_mask(weight, mask, blk):
    rows, cols = weight.shape
    shaped = weight.reshape(rows // blk, blk, cols // blk, blk)
    return (shaped * mask[:, None, :, None].astype(weight.dtype)).reshape(rows, cols)

def gelu_tanh(value):
    return jax.nn.gelu(value, approximate=True)

def reference(tokens, w_in, w_out, mask_in, mask_out, out_grad):
    win = apply_mask(w_in, mask_in, BLK)
    wout = apply_mask(w_out, mask_out, BLK)
    hidden = jnp.dot(tokens, win, preferred_element_type=jnp.float32)
    act = gelu_tanh(hidden).astype(jnp.bfloat16)
    mixed = jnp.dot(act, wout, preferred_element_type=jnp.float32).astype(jnp.bfloat16)
    act_grad = jnp.dot(out_grad, wout.T, preferred_element_type=jnp.float32)
    unused, pull = jax.vjp(gelu_tanh, hidden)
    hid_grad = pull(act_grad)[0].astype(jnp.bfloat16)
    w_out_grad = apply_mask(jnp.dot(act.T, out_grad, preferred_element_type=jnp.float32), mask_out, BLK).astype(jnp.bfloat16)
    tokens_grad = jnp.dot(hid_grad, win.T, preferred_element_type=jnp.float32).astype(jnp.bfloat16)
    w_in_grad = apply_mask(jnp.dot(tokens.T, hid_grad, preferred_element_type=jnp.float32), mask_in, BLK).astype(jnp.bfloat16)
    return (mixed, tokens_grad, w_in_grad, w_out_grad)
```

```python
import functools
import math

import jax
import jax.numpy as jnp
from jax import lax
from jax.experimental import pallas as pl
from jax.experimental.pallas import tpu as pltpu
from jax.sharding import PartitionSpec as P

BLK = 128
SUB = 16
MESH = pl.DeviceIdType.MESH
VMEM = pl.BlockSpec(memory_space=pltpu.VMEM)
DMA = pltpu.SemaphoreType.DMA
COLS, SPAN, STEP = 512, 512, 512
GELU_A, GELU_B = 0.7978845608028654, 0.044715


def remote(src, dst, send, recv, axis, device):
    return pltpu.make_async_remote_copy(
        src_ref=src, dst_ref=dst, send_sem=send, recv_sem=recv,
        device_id={axis: device}, device_id_type=MESH,
    )


def spread(mask, start, count):
    rows, cols = mask.shape

    def repeats(shape, dim, size, offset):
        apart = lax.broadcasted_iota(jnp.int32, shape, dim) - size * (
            lax.broadcasted_iota(jnp.int32, shape, 1 - dim) - offset
        )
        return jnp.where((apart >= 0) & (apart < size), 1.0, 0.0).astype(jnp.bfloat16)

    flags = mask.astype(jnp.float32).astype(jnp.bfloat16)
    tall = jnp.dot(repeats((count * SUB, rows), 0, SUB, start), flags, preferred_element_type=jnp.float32)
    wide = jnp.dot(tall.astype(jnp.bfloat16), repeats((cols, cols * BLK), 1, BLK, 0), preferred_element_type=jnp.float32)
    return wide.astype(jnp.bfloat16)


def masked(weight, flags):
    rows, cols = weight.shape
    shaped = weight.reshape(rows // BLK, BLK // SUB, SUB, cols)
    return (shaped * flags.reshape(rows // BLK, 1, SUB, cols)).reshape(rows, cols)


def cut(width, most):
    return next(width // count for count in range(1, width // BLK + 1)
                if width % (count * BLK) == 0 and width // count <= most)


def gelu_parts(value):
    square = value * value
    tanh = jnp.tanh(GELU_A * (value + GELU_B * (square * value)))
    half = 0.5 * (1.0 + tanh)
    slope = half + 0.5 * value * (1.0 - tanh * tanh) * (GELU_A * (1.0 + (3.0 * GELU_B) * square))
    return value * half, slope


def layer_kernel(far, near, chips, cores, *refs):
    srcs, masks, weights = refs[:2], refs[2:4], refs[4:6]
    tokens_t, act_t, hid, grad_rows, mixed, tokens_grad = refs[6:12]
    flags, held, loaded, token_rows, act = refs[12:14], refs[14:16], refs[16:18], refs[18], refs[19]
    zs, zr, ys, yr, own = refs[20:25]
    parts, pair, sums, landed, slopes, ps, pr, xs, xr, gs, gr = refs[25:36]
    wide, short, over, near_sums, far_parts, cys, cyr, czs, czr = refs[36:]
    dsts, sides = (token_rows, grad_rows), (act, hid)
    results = (mixed, tokens_grad)
    mine = lax.axis_index("col")
    z, y = mine // near, lax.rem(mine, near)
    rows_z = [lax.rem(z + d, far) for d in range(1, far)]
    rows_y = [lax.rem(y + e, near) for e in range(1, near)]
    along_z = [r * near + y for r in rows_z]
    along_y = [z * near + r for r in rows_y]
    me = lax.axis_index("row")
    x, k = me // cores, lax.rem(me, cores)
    partner = x * cores + (1 - k)
    peers = [lax.rem(x + d, chips) * cores + k for d in range(1, chips)]
    pieces, cols = parts.shape[1], parts.shape[-1]
    chunks, span = wide.shape[1], wide.shape[-1]
    shaped = wide.shape[2:5]
    sent = []

    def push(copy):
        copy.start()
        sent.append(copy)

    def load(a, p):
        spot = pl.ds(p * cols, cols)
        if a == 0:
            return pltpu.make_async_copy(weights[0].at[:, spot], held[0].at[:, spot], loaded[0].at[p])
        return pltpu.make_async_copy(weights[1].at[spot, :], held[1].at[spot, :], loaded[1].at[p])

    for p in range(pieces):
        load(0, p).start()
    barrier = pltpu.get_barrier_semaphore()
    for axis, group in (("col", along_z + along_y), ("row", [partner] + peers)):
        for peer in group:
            pl.semaphore_signal(barrier, inc=1, device_id={axis: peer}, device_id_type=MESH)
    pl.semaphore_wait(barrier, len(along_z) + len(along_y) + len(peers) + 1)

    def give(a):
        for e, peer in enumerate(along_y):
            push(remote(srcs[a], dsts[a].at[mine], ys.at[a, 0, e], yr.at[a, 0, e], "col", peer))
        for d, peer in enumerate(along_z):
            push(remote(srcs[a], dsts[a].at[mine], zs.at[a, d], zr.at[a, d], "col", peer))

    def relay(a, d):
        slot = dsts[a].at[lax.rem(z + far - d - 1, far) * near + y]
        remote(srcs[a], slot, zs.at[a, d], zr.at[a, d], "col", along_z[d]).wait_recv()
        for e, peer in enumerate(along_y):
            push(remote(slot, slot, ys.at[a, d + 1, e], yr.at[a, d + 1, e], "col", peer))

    def gathered(a):
        for d in range(far):
            for e in range(near - 1):
                slot = dsts[a].at[lax.rem(z + far - d, far) * near + lax.rem(y + near - e - 1, near)]
                remote(slot, slot, ys.at[a, d, e], yr.at[a, d, e], "col", along_y[e]).wait_recv()
        kept[a].wait()

    def rows_of(ref):
        return ref[...].reshape(-1, ref.shape[-1])

    def ahead(left, a, start, size):
        spot = pl.ds(start, size)
        return jnp.dot(left, masked(held[a][:, spot], flags[a][:, spot]), preferred_element_type=jnp.float32)

    def back(right, a, start, size):
        spot, marks = pl.ds(start, size), pl.ds(start // BLK * SUB, size // BLK * SUB)
        turned = lax.dot_general(
            masked(held[a][spot, :], flags[a][marks, :]), right, (((1,), (1,)), ((), ())),
            preferred_element_type=jnp.float32,
        )
        return turned.T

    def to_partner(a, p):
        return remote(parts.at[a, p, 1 - k], pair.at[a, p], ps.at[a, p], pr.at[a, p], "row", partner)

    def to_chip(a, p, d):
        return remote(sums.at[a, p], landed.at[a, p, d], xs.at[a, p, d], xr.at[a, p, d], "row", peers[d])

    def give_partner(a, p, owner):
        share = sides[a].at[owner, :, pl.ds(p * cols, cols)]
        return remote(share, share, gs.at[a, p], gr.at[a, p], "row", partner)

    def compute(a, p):
        load(a, p).wait()
        value = (ahead if a == 0 else back)(rows_of(dsts[a]), a, p * cols, cols)
        parts[a, p] = value.reshape(parts.shape[2:])
        push(to_partner(a, p))

    def reduce_pair(a, p):
        to_partner(a, p).wait_recv()
        total = parts[a, p, k] + pair[a, p]
        pair[a, p] = total
        sums[a, p] = total.astype(sums.dtype)
        for d in range(chips - 1):
            push(to_chip(a, p, d))

    def finish(a, p):
        total = pair[a, p]
        for d in range(chips - 1):
            to_chip(a, p, d).wait_recv()
            total = total + landed[a, p, d].astype(jnp.float32)
        if a == 0:
            value, slopes[p] = gelu_parts(total)
        else:
            value = total * slopes[p]
        sides[a][k, :, pl.ds(p * cols, cols)] = value.astype(sides[a].dtype)
        push(give_partner(a, p, k))

    def arrive(a):
        for p in range(pieces):
            give_partner(a, p, 1 - k).wait_recv()

    def over_y(a, q, e):
        return remote(short.at[a, q, :, rows_y[e]], over.at[a, q, e], cys.at[a, q, e], cyr.at[a, q, e], "col", along_y[e])

    def over_z(a, q, d):
        return remote(near_sums.at[a, q, d], far_parts.at[a, q, d], czs.at[a, q, d], czr.at[a, q, d], "col", along_z[d])

    def near_sum(a, q, row):
        total = wide[a, q, row, y]
        for e in range(near - 1):
            total = total + over[a, q, e, row].astype(jnp.float32)
        return total

    def output(a, q):
        value = (ahead if a == 0 else back)(rows_of(sides[a]), 1 - a, q * span, span)
        laid = value.reshape(*shaped, span)
        wide[a, q] = laid
        short[a, q] = laid.astype(short.dtype)
        for e in range(near - 1):
            push(over_y(a, q, e))

    def reduce_near(a, q):
        for e in range(near - 1):
            over_y(a, q, e).wait_recv()
        for d in range(far - 1):
            near_sums[a, q, d] = near_sum(a, q, rows_z[d]).astype(near_sums.dtype)
            push(over_z(a, q, d))

    def settle(a, q):
        total = near_sum(a, q, z)
        for d in range(far - 1):
            over_z(a, q, d).wait_recv()
            total = total + far_parts[a, q, d].astype(jnp.float32)
        results[a][:, pl.ds(q * span, span)] = total.astype(results[a].dtype)

    give(0)
    kept = [pltpu.make_async_copy(srcs[a], dsts[a].at[mine], own.at[a]) for a in range(2)]
    for copy in kept:
        copy.start()
    for a in range(2):
        flags[a][...] = spread(masks[a][...], 0, masks[a].shape[0])
    for d in range(far - 1):
        relay(0, d)
    give(1)
    for p in range(pieces):
        load(1, p).start()
    gathered(0)

    def spaced(main, side):
        done = 0
        for n, job in enumerate(main):
            job()
            upto = (n + 1) * len(side) // len(main)
            for other in side[done:upto]:
                other()
            done = upto

    call = functools.partial
    relays = [call(relay, 1, d) for d in range(far - 1)]
    main = [call(compute, 0, 0)]
    for p in range(1, pieces):
        main += [call(compute, 0, p), call(reduce_pair, 0, p - 1)]
    main += [call(reduce_pair, 0, pieces - 1)]
    main += [call(finish, 0, p) for p in range(pieces)]
    spaced(main, relays)
    tokens_t[...] = rows_of(token_rows).T
    gathered(1)
    compute(1, 0)
    for p in range(1, pieces):
        compute(1, p)
        reduce_pair(1, p - 1)
    reduce_pair(1, pieces - 1)
    arrive(0)
    lead = [call(output, 0, 0)]
    for q in range(1, chunks):
        lead += [call(output, 0, q), call(reduce_near, 0, q - 1)]
    spaced(lead, [call(finish, 1, p) for p in range(pieces)])
    reduce_near(0, chunks - 1)
    act_t[...] = rows_of(act).T
    arrive(1)
    output(1, 0)
    for q in range(1, chunks):
        output(1, q)
        settle(0, q - 1)
        reduce_near(1, q - 1)
    settle(0, chunks - 1)
    reduce_near(1, chunks - 1)
    for q in range(chunks):
        settle(1, q)
    for copy in sent:
        copy.wait_send()


ANY = pl.BlockSpec(memory_space=pl.ANY)


def layer_stage(far, near, chips, cores, first, second, masks, down, up):
    depth, width = down.shape
    tokens = first.shape[0] * far * near
    cols, span = cut(width, COLS), cut(depth, SPAN)
    pieces, chunks = width // cols, depth // span
    half, share = tokens // cores, tokens // (far * near)
    full = (far * near,) + first.shape
    bf16, f32 = jnp.bfloat16, jnp.float32
    tokens_t, act_t, hid, grad_rows, mixed, tokens_grad = pl.pallas_call(
        functools.partial(layer_kernel, far, near, chips, cores),
        out_shape=(
            jax.ShapeDtypeStruct((depth, tokens), bf16), jax.ShapeDtypeStruct((width, tokens), bf16),
            jax.ShapeDtypeStruct((cores, half, width), bf16), jax.ShapeDtypeStruct(full, bf16),
            jax.ShapeDtypeStruct((share, depth), bf16), jax.ShapeDtypeStruct((share, depth), bf16),
        ),
        in_specs=[VMEM] * 4 + [ANY] * 2,
        out_specs=(VMEM,) * 6,
        scratch_shapes=[
            pltpu.VMEM((depth // BLK * SUB, width), bf16), pltpu.VMEM((width // BLK * SUB, depth), bf16),
            pltpu.VMEM((depth, width), bf16), pltpu.VMEM((width, depth), bf16), DMA((pieces,)), DMA((pieces,)),
            pltpu.VMEM(full, bf16), pltpu.VMEM((cores, half, width), bf16),
            DMA((2, far - 1)), DMA((2, far - 1)), DMA((2, far, near - 1)), DMA((2, far, near - 1)), DMA((2,)),
            pltpu.VMEM((2, pieces, cores, half, cols), f32), pltpu.VMEM((2, pieces, half, cols), f32),
            pltpu.VMEM((2, pieces, half, cols), bf16), pltpu.VMEM((2, pieces, chips - 1, half, cols), bf16),
            pltpu.VMEM((pieces, half, cols), f32),
            DMA((2, pieces)), DMA((2, pieces)),
            DMA((2, pieces, chips - 1)), DMA((2, pieces, chips - 1)),
            DMA((2, pieces)), DMA((2, pieces)),
            pltpu.VMEM((2, chunks, far, near, share, span), f32),
            pltpu.VMEM((2, chunks, far, near, share, span), bf16),
            pltpu.VMEM((2, chunks, near - 1, far, share, span), bf16),
            pltpu.VMEM((2, chunks, far - 1, share, span), bf16),
            pltpu.VMEM((2, chunks, far - 1, share, span), bf16),
            DMA((2, chunks, near - 1)), DMA((2, chunks, near - 1)),
            DMA((2, chunks, far - 1)), DMA((2, chunks, far - 1)),
        ],
        compiler_params=pltpu.CompilerParams(
            collective_id=0, has_side_effects=True, vmem_limit_bytes=67043328
        ),
        name="layer_stage",
    )(first, second, *masks, down, up)
    flat = lambda each: each.reshape(tokens, each.shape[-1])
    return tokens_t, act_t, flat(hid), flat(grad_rows), mixed, tokens_grad


def outer_kernel(tokens_ref, hid_ref, in_mask, act_ref, grad_ref, out_mask, mixed_ref, back_ref, *outs):
    in_ref, out_ref, mixed_out, back_out = outs
    step = pl.program_id(0)

    @pl.when(step == 0)
    def _():
        mixed_out[...] = mixed_ref[...]
        back_out[...] = back_ref[...]

    def one(left, right, mask, out):
        count = out.shape[0] // BLK
        full = jnp.dot(left[...], right[...], preferred_element_type=jnp.float32)
        out[...] = masked(full.astype(out.dtype), spread(mask[...], step * count, count))

    one(tokens_ref, hid_ref, in_mask, in_ref)
    one(act_ref, grad_ref, out_mask, out_ref)


def outers(tokens, hid, in_mask, act, grad, out_mask, mixed, back):
    depth, count = tokens.shape
    width = hid.shape[1]
    steps = math.gcd(depth // BLK, width // BLK)
    while steps % 2 == 0 and depth // steps < STEP:
        steps //= 2
    down, up = depth // steps, width // steps
    whole = lambda each: pl.BlockSpec(each.shape, lambda i: (0, 0))
    same = lambda each: jax.ShapeDtypeStruct(each.shape, each.dtype)
    return pl.pallas_call(
        outer_kernel,
        grid=(steps,),
        out_shape=[
            jax.ShapeDtypeStruct((depth, width), jnp.bfloat16), jax.ShapeDtypeStruct((width, depth), jnp.bfloat16),
            same(mixed), same(back),
        ],
        in_specs=[
            pl.BlockSpec((down, count), lambda i: (i, 0)), whole(hid), whole(in_mask),
            pl.BlockSpec((up, count), lambda i: (i, 0)), whole(grad), whole(out_mask),
            whole(mixed), whole(back),
        ],
        out_specs=[
            pl.BlockSpec((down, width), lambda i: (i, 0)), pl.BlockSpec((up, depth), lambda i: (i, 0)),
            whole(mixed), whole(back),
        ],
        name="outers",
    )(tokens, hid, in_mask, act, grad, out_mask, mixed, back)


def local(far, near, chips, cores, tokens, w_in, w_out, mask_in, mask_out, out_grad):
    tokens_t, act_t, hid, grad_rows, mixed, tokens_grad = layer_stage(
        far, near, chips, cores, tokens, out_grad, (mask_in, mask_out), w_in, w_out
    )
    w_in_grad, w_out_grad, mixed, tokens_grad = outers(
        tokens_t, hid, mask_in, act_t, grad_rows, mask_out, mixed, tokens_grad
    )
    return (mixed, tokens_grad, w_in_grad, w_out_grad)


def solution(mesh):
    columns, rows = mesh.shape["col"], mesh.shape["row"]
    near = 2 ** (int(math.log2(columns)) // 2)
    return jax.shard_map(
        functools.partial(local, columns // near, near, rows // 2, 2),
        mesh=mesh,
        in_specs=(
            P("col", "row"),
            P("row", "col"),
            P("col", "row"),
            P("row", "col"),
            P("col", "row"),
            P("col", "row"),
        ),
        out_specs=(P("col", "row"), P("col", "row"), P("row", "col"), P("col", "row")),
        check_vma=False,
    )
```

```python
import functools
import math

import jax
import jax.numpy as jnp
from jax import lax
from jax.experimental import pallas as pl
from jax.experimental.pallas import tpu as pltpu
from jax.sharding import PartitionSpec as P

BLK = 128
SUB = 16
MESH = pl.DeviceIdType.MESH
VMEM = pl.BlockSpec(memory_space=pltpu.VMEM)
SMEM = pl.BlockSpec(memory_space=pltpu.SMEM)
DMA = pltpu.SemaphoreType.DMA
COLS, SPAN, STEP = 512, 512, 512
GELU_A, GELU_B = 0.7978845608028654, 0.044715


def remote(src, dst, send, recv, axis, device):
    return pltpu.make_async_remote_copy(
        src_ref=src, dst_ref=dst, send_sem=send, recv_sem=recv,
        device_id={axis: device}, device_id_type=MESH,
    )


def spread(mask):
    rows, cols = mask.shape

    def repeats(shape, dim, size):
        apart = lax.broadcasted_iota(jnp.int32, shape, dim) - size * lax.broadcasted_iota(jnp.int32, shape, 1 - dim)
        return jnp.where((apart >= 0) & (apart < size), 1.0, 0.0).astype(jnp.bfloat16)

    flags = mask.astype(jnp.float32).astype(jnp.bfloat16)
    tall = jnp.dot(repeats((rows * SUB, rows), 0, SUB), flags, preferred_element_type=jnp.float32)
    wide = jnp.dot(tall.astype(jnp.bfloat16), repeats((cols, cols * BLK), 1, BLK), preferred_element_type=jnp.float32)
    return wide.astype(jnp.bfloat16)


def masked(weight, flags):
    rows, cols = weight.shape
    shaped = weight.reshape(rows // BLK, BLK // SUB, SUB, cols)
    return (shaped * flags.reshape(rows // BLK, 1, SUB, cols)).reshape(rows, cols)


def cut(width, most):
    return next(width // count for count in range(1, width // BLK + 1)
                if width % (count * BLK) == 0 and width // count <= most)


def gelu_parts(value):
    square = value * value
    tanh = jnp.tanh(GELU_A * (value + GELU_B * (square * value)))
    half = 0.5 * (1.0 + tanh)
    slope = half + 0.5 * value * (1.0 - tanh * tanh) * (GELU_A * (1.0 + (3.0 * GELU_B) * square))
    return value * half, slope


def layer_kernel(far, near, chips, cores, *refs):
    srcs, masks, weights = refs[:2], refs[2:4], refs[4:6]
    tokens_t, act_t, hid, grad_rows, mixed, tokens_grad = refs[6:12]
    flags, held, loaded, token_rows, act = refs[12:14], refs[14:16], refs[16:18], refs[18], refs[19]
    zs, zr, ys, yr, own = refs[20:25]
    parts, pair, sums, landed, slopes, ps, pr, xs, xr, gs, gr = refs[25:36]
    wide, short, over, near_sums, far_parts, cys, cyr, czs, czr = refs[36:]
    dsts, sides = (token_rows, grad_rows), (act, hid)
    results = (mixed, tokens_grad)
    mine = lax.axis_index("col")
    z, y = mine // near, lax.rem(mine, near)
    rows_z = [lax.rem(z + d, far) for d in range(1, far)]
    rows_y = [lax.rem(y + e, near) for e in range(1, near)]
    along_z = [r * near + y for r in rows_z]
    along_y = [z * near + r for r in rows_y]
    me = lax.axis_index("row")
    x, k = me // cores, lax.rem(me, cores)
    partner = x * cores + (1 - k)
    peers = [lax.rem(x + d, chips) * cores + k for d in range(1, chips)]
    pieces, cols = parts.shape[1], parts.shape[-1]
    chunks, span = wide.shape[1], wide.shape[-1]
    shaped = wide.shape[2:5]
    sent = []

    def push(copy):
        copy.start()
        sent.append(copy)

    def load(a, p):
        spot = pl.ds(p * cols, cols)
        if a == 0:
            return pltpu.make_async_copy(weights[0].at[:, spot], held[0].at[:, spot], loaded[0].at[p])
        return pltpu.make_async_copy(weights[1].at[spot, :], held[1].at[spot, :], loaded[1].at[p])

    for p in range(pieces):
        load(0, p).start()
    barrier = pltpu.get_barrier_semaphore()
    for axis, group in (("col", along_z + along_y), ("row", [partner] + peers)):
        for peer in group:
            pl.semaphore_signal(barrier, inc=1, device_id={axis: peer}, device_id_type=MESH)
    pl.semaphore_wait(barrier, len(along_z) + len(along_y) + len(peers) + 1)

    def near_give(a):
        for e, peer in enumerate(along_y):
            push(remote(srcs[a], dsts[a].at[mine], ys.at[a, 0, e], yr.at[a, 0, e], "col", peer))

    def far_give(a):
        for d, peer in enumerate(along_z):
            push(remote(srcs[a], dsts[a].at[mine], zs.at[a, d], zr.at[a, d], "col", peer))

    def relay(a, d):
        slot = dsts[a].at[lax.rem(z + far - d - 1, far) * near + y]
        remote(srcs[a], slot, zs.at[a, d], zr.at[a, d], "col", along_z[d]).wait_recv()
        for e, peer in enumerate(along_y):
            push(remote(slot, slot, ys.at[a, d + 1, e], yr.at[a, d + 1, e], "col", peer))

    def gathered(a):
        for d in range(far):
            for e in range(near - 1):
                slot = dsts[a].at[lax.rem(z + far - d, far) * near + lax.rem(y + near - e - 1, near)]
                remote(slot, slot, ys.at[a, d, e], yr.at[a, d, e], "col", along_y[e]).wait_recv()
        kept[a].wait()

    def rows_of(ref):
        return ref[...].reshape(-1, ref.shape[-1])

    def ahead(left, a, start, size):
        spot = pl.ds(start, size)
        return jnp.dot(left, masked(held[a][:, spot], flags[a][:, spot]), preferred_element_type=jnp.float32)

    def back(right, a, start, size):
        spot, marks = pl.ds(start, size), pl.ds(start // BLK * SUB, size // BLK * SUB)
        turned = lax.dot_general(
            masked(held[a][spot, :], flags[a][marks, :]), right, (((1,), (1,)), ((), ())),
            preferred_element_type=jnp.float32,
        )
        return turned.T

    def to_partner(a, p):
        return remote(parts.at[a, p, 1 - k], pair.at[a, p], ps.at[a, p], pr.at[a, p], "row", partner)

    def to_chip(a, p, d):
        return remote(sums.at[a, p], landed.at[a, p, d], xs.at[a, p, d], xr.at[a, p, d], "row", peers[d])

    def give_partner(a, p, owner):
        share = sides[a].at[owner, :, pl.ds(p * cols, cols)]
        return remote(share, share, gs.at[a, p], gr.at[a, p], "row", partner)

    def compute(a, p):
        load(a, p).wait()
        value = (ahead if a == 0 else back)(rows_of(dsts[a]), a, p * cols, cols)
        parts[a, p] = value.reshape(parts.shape[2:])
        push(to_partner(a, p))

    def reduce_pair(a, p):
        to_partner(a, p).wait_recv()
        total = parts[a, p, k] + pair[a, p]
        pair[a, p] = total
        sums[a, p] = total.astype(sums.dtype)
        for d in range(chips - 1):
            push(to_chip(a, p, d))

    def finish(a, p):
        total = pair[a, p]
        for d in range(chips - 1):
            to_chip(a, p, d).wait_recv()
            total = total + landed[a, p, d].astype(jnp.float32)
        if a == 0:
            value, slopes[p] = gelu_parts(total)
        else:
            value = total * slopes[p]
        sides[a][k, :, pl.ds(p * cols, cols)] = value.astype(sides[a].dtype)
        push(give_partner(a, p, k))

    def arrive(a):
        for p in range(pieces):
            give_partner(a, p, 1 - k).wait_recv()

    def over_y(a, q, e):
        return remote(short.at[a, q, :, rows_y[e]], over.at[a, q, e], cys.at[a, q, e], cyr.at[a, q, e], "col", along_y[e])

    def over_z(a, q, d):
        return remote(near_sums.at[a, q, d], far_parts.at[a, q, d], czs.at[a, q, d], czr.at[a, q, d], "col", along_z[d])

    def near_sum(a, q, row):
        total = wide[a, q, row, y]
        for e in range(near - 1):
            total = total + over[a, q, e, row].astype(jnp.float32)
        return total

    def output(a, q):
        value = (ahead if a == 0 else back)(rows_of(sides[a]), 1 - a, q * span, span)
        laid = value.reshape(*shaped, span)
        wide[a, q] = laid
        short[a, q] = laid.astype(short.dtype)
        for e in range(near - 1):
            push(over_y(a, q, e))

    def reduce_near(a, q):
        for e in range(near - 1):
            over_y(a, q, e).wait_recv()
        for d in range(far - 1):
            near_sums[a, q, d] = near_sum(a, q, rows_z[d]).astype(near_sums.dtype)
            push(over_z(a, q, d))

    def settle(a, q):
        total = near_sum(a, q, z)
        for d in range(far - 1):
            over_z(a, q, d).wait_recv()
            total = total + far_parts[a, q, d].astype(jnp.float32)
        results[a][:, pl.ds(q * span, span)] = total.astype(results[a].dtype)

    near_give(0)
    far_give(0)
    kept = [pltpu.make_async_copy(srcs[a], dsts[a].at[mine], own.at[a]) for a in range(2)]
    for copy in kept:
        copy.start()
    far_give(1)
    for a in range(2):
        flags[a][...] = spread(masks[a][...])
    for d in range(far - 1):
        relay(0, d)
    near_give(1)
    for p in range(pieces):
        load(1, p).start()
    gathered(0)

    def run(jobs):
        for job in jobs:
            job()

    def merge(main, side, lag):
        side = list(side)
        for n, job in enumerate(main):
            job()
            if n >= lag and side:
                side.pop(0)()
        run(side)

    def turn(out, ref):
        out[...] = rows_of(ref).T

    call = functools.partial
    each = lambda job, a, count: [call(job, a, n) for n in range(count)]
    ends0, ends1 = each(finish, 0, pieces), each(finish, 1, pieces)
    outs0, outs1 = each(output, 0, chunks), each(output, 1, chunks)
    nears0, nears1 = each(reduce_near, 0, chunks), each(reduce_near, 1, chunks)
    held_back = min(2, pieces - 1)
    merge(each(compute, 0, pieces), each(reduce_pair, 0, pieces), 2)
    run([call(relay, 1, d) for d in range(far - 1)])
    turn(tokens_t, token_rows)
    run(ends0[:pieces - held_back])
    gathered(1)
    turns = [call(compute, 1, 0)]
    for p in range(1, pieces):
        turns += [call(compute, 1, p), call(reduce_pair, 1, p - 1)]
    merge(turns + [call(reduce_pair, 1, pieces - 1)], ends0[pieces - held_back:], 3)
    arrive(0)
    merge(outs0, ends1[:pieces - held_back], 0)
    merge(ends1[pieces - held_back:], nears0[:held_back], 0)
    turn(act_t, act)
    arrive(1)
    merge(outs1, nears0[held_back:], 1)
    merge(nears1, each(settle, 0, chunks), 0)
    run(each(settle, 1, chunks))
    for copy in sent:
        copy.wait_send()


ANY = pl.BlockSpec(memory_space=pl.ANY)


def layer_stage(far, near, chips, cores, first, second, masks, down, up):
    depth, width = down.shape
    tokens = first.shape[0] * far * near
    cols, span = cut(width, COLS), cut(depth, SPAN)
    pieces, chunks = width // cols, depth // span
    half, share = tokens // cores, tokens // (far * near)
    full = (far * near,) + first.shape
    bf16, f32 = jnp.bfloat16, jnp.float32
    tokens_t, act_t, hid, grad_rows, mixed, tokens_grad = pl.pallas_call(
        functools.partial(layer_kernel, far, near, chips, cores),
        out_shape=(
            jax.ShapeDtypeStruct((depth, tokens), bf16), jax.ShapeDtypeStruct((width, tokens), bf16),
            jax.ShapeDtypeStruct((cores, half, width), bf16), jax.ShapeDtypeStruct(full, bf16),
            jax.ShapeDtypeStruct((share, depth), bf16), jax.ShapeDtypeStruct((share, depth), bf16),
        ),
        in_specs=[VMEM] * 4 + [ANY] * 2,
        out_specs=(VMEM,) * 6,
        scratch_shapes=[
            pltpu.VMEM((depth // BLK * SUB, width), bf16), pltpu.VMEM((width // BLK * SUB, depth), bf16),
            pltpu.VMEM((depth, width), bf16), pltpu.VMEM((width, depth), bf16), DMA((pieces,)), DMA((pieces,)),
            pltpu.VMEM(full, bf16), pltpu.VMEM((cores, half, width), bf16),
            DMA((2, far - 1)), DMA((2, far - 1)), DMA((2, far, near - 1)), DMA((2, far, near - 1)), DMA((2,)),
            pltpu.VMEM((2, pieces, cores, half, cols), f32), pltpu.VMEM((2, pieces, half, cols), f32),
            pltpu.VMEM((2, pieces, half, cols), bf16), pltpu.VMEM((2, pieces, chips - 1, half, cols), bf16),
            pltpu.VMEM((pieces, half, cols), f32),
            DMA((2, pieces)), DMA((2, pieces)),
            DMA((2, pieces, chips - 1)), DMA((2, pieces, chips - 1)),
            DMA((2, pieces)), DMA((2, pieces)),
            pltpu.VMEM((2, chunks, far, near, share, span), f32),
            pltpu.VMEM((2, chunks, far, near, share, span), bf16),
            pltpu.VMEM((2, chunks, near - 1, far, share, span), bf16),
            pltpu.VMEM((2, chunks, far - 1, share, span), bf16),
            pltpu.VMEM((2, chunks, far - 1, share, span), bf16),
            DMA((2, chunks, near - 1)), DMA((2, chunks, near - 1)),
            DMA((2, chunks, far - 1)), DMA((2, chunks, far - 1)),
        ],
        compiler_params=pltpu.CompilerParams(
            collective_id=0, has_side_effects=True, vmem_limit_bytes=67043328
        ),
        name="layer_stage",
    )(first, second, *masks, down, up)
    flat = lambda each: each.reshape(tokens, each.shape[-1])
    return tokens_t, act_t, flat(hid), flat(grad_rows), mixed, tokens_grad


def outer_kernel(tokens_ref, hid_ref, in_mask, act_ref, grad_ref, out_mask, mixed_ref, back_ref, *outs):
    in_ref, out_ref, mixed_out, back_out = outs
    step = pl.program_id(0)

    @pl.when(step == 0)
    def _():
        mixed_out[...] = mixed_ref[...]
        back_out[...] = back_ref[...]

    def one(left, right, mask, out):
        down, across = out.shape[0] // BLK, out.shape[1] // BLK
        full = jnp.dot(left[...], right[...], preferred_element_type=jnp.float32)
        for b in range(down):
            for c in range(across):
                block = slice(b * BLK, (b + 1) * BLK), slice(c * BLK, (c + 1) * BLK)
                out[block] = (full[block] * mask[step * down + b, c].astype(jnp.float32)).astype(out.dtype)

    one(tokens_ref, hid_ref, in_mask, in_ref)
    one(act_ref, grad_ref, out_mask, out_ref)


def outers(tokens, hid, in_mask, act, grad, out_mask, mixed, back):
    depth, count = tokens.shape
    width = hid.shape[1]
    steps = math.gcd(depth // BLK, width // BLK)
    while steps % 2 == 0 and depth // steps < STEP:
        steps //= 2
    down, up = depth // steps, width // steps
    whole = lambda each: pl.BlockSpec(each.shape, lambda i: (0, 0))
    same = lambda each: jax.ShapeDtypeStruct(each.shape, each.dtype)
    return pl.pallas_call(
        outer_kernel,
        grid=(steps,),
        out_shape=[
            jax.ShapeDtypeStruct((depth, width), jnp.bfloat16), jax.ShapeDtypeStruct((width, depth), jnp.bfloat16),
            same(mixed), same(back),
        ],
        in_specs=[
            pl.BlockSpec((down, count), lambda i: (i, 0)), whole(hid), SMEM,
            pl.BlockSpec((up, count), lambda i: (i, 0)), whole(grad), SMEM,
            whole(mixed), whole(back),
        ],
        out_specs=[
            pl.BlockSpec((down, width), lambda i: (i, 0)), pl.BlockSpec((up, depth), lambda i: (i, 0)),
            whole(mixed), whole(back),
        ],
        name="outers",
    )(tokens, hid, in_mask, act, grad, out_mask, mixed, back)


def local(far, near, chips, cores, tokens, w_in, w_out, mask_in, mask_out, out_grad):
    tokens_t, act_t, hid, grad_rows, mixed, tokens_grad = layer_stage(
        far, near, chips, cores, tokens, out_grad, (mask_in, mask_out), w_in, w_out
    )
    w_in_grad, w_out_grad, mixed, tokens_grad = outers(
        tokens_t, hid, mask_in, act_t, grad_rows, mask_out, mixed, tokens_grad
    )
    return (mixed, tokens_grad, w_in_grad, w_out_grad)


def solution(mesh):
    columns, rows = mesh.shape["col"], mesh.shape["row"]
    near = 2 ** (int(math.log2(columns)) // 2)
    return jax.shard_map(
        functools.partial(local, columns // near, near, rows // 2, 2),
        mesh=mesh,
        in_specs=(
            P("col", "row"),
            P("row", "col"),
            P("col", "row"),
            P("row", "col"),
            P("col", "row"),
            P("col", "row"),
        ),
        out_specs=(P("col", "row"), P("col", "row"), P("row", "col"), P("col", "row")),
        check_vma=False,
    )
```

```python
import functools
import math

import jax
import jax.numpy as jnp
from jax import lax
from jax.experimental import pallas as pl
from jax.experimental.pallas import tpu as pltpu
from jax.sharding import PartitionSpec as P

BLK = 128
SUB = 16
MESH = pl.DeviceIdType.MESH
VMEM = pl.BlockSpec(memory_space=pltpu.VMEM)
SMEM = pl.BlockSpec(memory_space=pltpu.SMEM)
DMA = pltpu.SemaphoreType.DMA
COLS, SPAN, STEP = 512, 512, 512
GELU_A, GELU_B = 0.7978845608028654, 0.044715


def remote(src, dst, send, recv, axis, device):
    return pltpu.make_async_remote_copy(
        src_ref=src, dst_ref=dst, send_sem=send, recv_sem=recv,
        device_id={axis: device}, device_id_type=MESH,
    )


def spread(mask):
    rows, cols = mask.shape

    def repeats(shape, dim, size):
        apart = lax.broadcasted_iota(jnp.int32, shape, dim) - size * lax.broadcasted_iota(jnp.int32, shape, 1 - dim)
        return jnp.where((apart >= 0) & (apart < size), 1.0, 0.0).astype(jnp.bfloat16)

    flags = mask.astype(jnp.float32).astype(jnp.bfloat16)
    tall = jnp.dot(repeats((rows * SUB, rows), 0, SUB), flags, preferred_element_type=jnp.float32)
    wide = jnp.dot(tall.astype(jnp.bfloat16), repeats((cols, cols * BLK), 1, BLK), preferred_element_type=jnp.float32)
    return wide.astype(jnp.bfloat16)


def masked(weight, flags):
    rows, cols = weight.shape
    shaped = weight.reshape(rows // BLK, BLK // SUB, SUB, cols)
    return (shaped * flags.reshape(rows // BLK, 1, SUB, cols)).reshape(rows, cols)


def cut(width, most):
    return next(width // count for count in range(1, width // BLK + 1)
                if width % (count * BLK) == 0 and width // count <= most)


def gelu_parts(value):
    square = value * value
    tanh = jnp.tanh(GELU_A * (value + GELU_B * (square * value)))
    half = 0.5 * (1.0 + tanh)
    slope = half + 0.5 * value * (1.0 - tanh * tanh) * (GELU_A * (1.0 + (3.0 * GELU_B) * square))
    return value * half, slope


def layer_kernel(far, near, chips, cores, *refs):
    srcs, mask_refs, weights = refs[:2], refs[2:4], refs[4:6]
    tokens_out, act_out, hid_out, grad_out, mixed, tokens_grad = refs[6:12]
    refs, extra = refs[:-8], refs[-8:]
    tokens_t, act_t, hid, grad_rows, *masks, read, saved = extra
    flags, held, loaded, token_rows, act = refs[12:14], refs[14:16], refs[16:18], refs[18], refs[19]
    zs, zr, ys, yr, own = refs[20:25]
    parts, pair, sums, landed, slopes, ps, pr, xs, xr, gs, gr = refs[25:36]
    wide, short, over, near_sums, far_parts, cys, cyr, czs, czr = refs[36:]
    dsts, sides = (token_rows, grad_rows), (act, hid)
    results = (mixed, tokens_grad)
    mine = lax.axis_index("col")
    z, y = mine // near, lax.rem(mine, near)
    rows_z = [lax.rem(z + d, far) for d in range(1, far)]
    rows_y = [lax.rem(y + e, near) for e in range(1, near)]
    along_z = [r * near + y for r in rows_z]
    along_y = [z * near + r for r in rows_y]
    me = lax.axis_index("row")
    x, k = me // cores, lax.rem(me, cores)
    partner = x * cores + (1 - k)
    peers = [lax.rem(x + d, chips) * cores + k for d in range(1, chips)]
    pieces, cols = parts.shape[1], parts.shape[-1]
    chunks, span = wide.shape[1], wide.shape[-1]
    shaped = wide.shape[2:5]
    sent = []

    def push(copy):
        copy.start()
        sent.append(copy)

    def load(a, p):
        spot = pl.ds(p * cols, cols)
        if a == 0:
            return pltpu.make_async_copy(weights[0].at[:, spot], held[0].at[:, spot], loaded[0].at[p])
        return pltpu.make_async_copy(weights[1].at[spot, :], held[1].at[spot, :], loaded[1].at[p])

    reads = [pltpu.make_async_copy(mask_refs[a], masks[a], read.at[a]) for a in range(2)]
    for copy in reads:
        copy.start()
    for p in range(pieces):
        load(0, p).start()
    barrier = pltpu.get_barrier_semaphore()
    for axis, group in (("col", along_z + along_y), ("row", [partner] + peers)):
        for peer in group:
            pl.semaphore_signal(barrier, inc=1, device_id={axis: peer}, device_id_type=MESH)
    pl.semaphore_wait(barrier, len(along_z) + len(along_y) + len(peers) + 1)

    def near_give(a):
        for e, peer in enumerate(along_y):
            push(remote(srcs[a], dsts[a].at[mine], ys.at[a, 0, e], yr.at[a, 0, e], "col", peer))

    def far_give(a):
        for d, peer in enumerate(along_z):
            push(remote(srcs[a], dsts[a].at[mine], zs.at[a, d], zr.at[a, d], "col", peer))

    def relay(a, d):
        slot = dsts[a].at[lax.rem(z + far - d - 1, far) * near + y]
        remote(srcs[a], slot, zs.at[a, d], zr.at[a, d], "col", along_z[d]).wait_recv()
        for e, peer in enumerate(along_y):
            push(remote(slot, slot, ys.at[a, d + 1, e], yr.at[a, d + 1, e], "col", peer))

    def gathered(a):
        for d in range(far):
            for e in range(near - 1):
                slot = dsts[a].at[lax.rem(z + far - d, far) * near + lax.rem(y + near - e - 1, near)]
                remote(slot, slot, ys.at[a, d, e], yr.at[a, d, e], "col", along_y[e]).wait_recv()
        kept[a].wait()

    def rows_of(ref):
        return ref[...].reshape(-1, ref.shape[-1])

    def ahead(left, a, start, size):
        spot = pl.ds(start, size)
        return jnp.dot(left, masked(held[a][:, spot], flags[a][:, spot]), preferred_element_type=jnp.float32)

    def back(right, a, start, size):
        spot, marks = pl.ds(start, size), pl.ds(start // BLK * SUB, size // BLK * SUB)
        turned = lax.dot_general(
            masked(held[a][spot, :], flags[a][marks, :]), right, (((1,), (1,)), ((), ())),
            preferred_element_type=jnp.float32,
        )
        return turned.T

    def to_partner(a, p):
        return remote(parts.at[a, p, 1 - k], pair.at[a, p], ps.at[a, p], pr.at[a, p], "row", partner)

    def to_chip(a, p, d):
        return remote(sums.at[a, p], landed.at[a, p, d], xs.at[a, p, d], xr.at[a, p, d], "row", peers[d])

    def give_partner(a, p, owner):
        share = sides[a].at[owner, :, pl.ds(p * cols, cols)]
        return remote(share, share, gs.at[a, p], gr.at[a, p], "row", partner)

    def compute(a, p):
        load(a, p).wait()
        value = (ahead if a == 0 else back)(rows_of(dsts[a]), a, p * cols, cols)
        parts[a, p] = value.reshape(parts.shape[2:])
        push(to_partner(a, p))

    def reduce_pair(a, p):
        to_partner(a, p).wait_recv()
        total = parts[a, p, k] + pair[a, p]
        pair[a, p] = total
        sums[a, p] = total.astype(sums.dtype)
        for d in range(chips - 1):
            push(to_chip(a, p, d))

    def finish(a, p):
        total = pair[a, p]
        for d in range(chips - 1):
            to_chip(a, p, d).wait_recv()
            total = total + landed[a, p, d].astype(jnp.float32)
        if a == 0:
            value, slopes[p] = gelu_parts(total)
        else:
            value = total * slopes[p]
        sides[a][k, :, pl.ds(p * cols, cols)] = value.astype(sides[a].dtype)
        push(give_partner(a, p, k))

    def arrive(a):
        for p in range(pieces):
            give_partner(a, p, 1 - k).wait_recv()

    def over_y(a, q, e):
        return remote(short.at[a, q, :, rows_y[e]], over.at[a, q, e], cys.at[a, q, e], cyr.at[a, q, e], "col", along_y[e])

    def over_z(a, q, d):
        return remote(near_sums.at[a, q, d], far_parts.at[a, q, d], czs.at[a, q, d], czr.at[a, q, d], "col", along_z[d])

    def near_sum(a, q, row):
        total = wide[a, q, row, y]
        for e in range(near - 1):
            total = total + over[a, q, e, row].astype(jnp.float32)
        return total

    def output(a, q):
        value = (ahead if a == 0 else back)(rows_of(sides[a]), 1 - a, q * span, span)
        laid = value.reshape(*shaped, span)
        wide[a, q] = laid
        short[a, q] = laid.astype(short.dtype)
        for e in range(near - 1):
            push(over_y(a, q, e))

    def reduce_near(a, q):
        for e in range(near - 1):
            over_y(a, q, e).wait_recv()
        for d in range(far - 1):
            near_sums[a, q, d] = near_sum(a, q, rows_z[d]).astype(near_sums.dtype)
            push(over_z(a, q, d))

    def settle(a, q):
        total = near_sum(a, q, z)
        for d in range(far - 1):
            over_z(a, q, d).wait_recv()
            total = total + far_parts[a, q, d].astype(jnp.float32)
        results[a][:, pl.ds(q * span, span)] = total.astype(results[a].dtype)

    near_give(0)
    far_give(0)
    near_give(1)
    kept = [pltpu.make_async_copy(srcs[a], dsts[a].at[mine], own.at[a]) for a in range(2)]
    for copy in kept:
        copy.start()
    far_give(1)
    for a in range(2):
        reads[a].wait()
        flags[a][...] = spread(masks[a][...])
    for d in range(far - 1):
        relay(0, d)
    for p in range(pieces):
        load(1, p).start()
    gathered(0)

    def run(jobs):
        for job in jobs:
            job()

    def merge(main, side, lag):
        side = list(side)
        for n, job in enumerate(main):
            job()
            if n >= lag and side:
                side.pop(0)()
        run(side)

    stored = [
        pltpu.make_async_copy(own_ref, out, saved.at[n])
        for n, (own_ref, out) in enumerate(((act_t, act_out), (hid, hid_out), (tokens_t, tokens_out), (grad_rows, grad_out)))
    ]

    def keep(n, turned, ref):
        turned[...] = rows_of(ref).T
        stored[n].start()

    call = functools.partial
    each = lambda job, a, count: [call(job, a, n) for n in range(count)]
    ends0, ends1 = each(finish, 0, pieces), each(finish, 1, pieces)
    outs0, outs1 = each(output, 0, chunks), each(output, 1, chunks)
    nears0, nears1 = each(reduce_near, 0, chunks), each(reduce_near, 1, chunks)
    held_back = min(2, pieces - 1)
    relay(1, 0)
    rest = [call(relay, 1, d) for d in range(1, far - 1)]
    turns = []
    for p in range(pieces):
        turns += [call(compute, 0, p)] + [call(reduce_pair, 0, p - 2)] * (p > 1)
    turns += [call(reduce_pair, 0, p) for p in range(max(0, pieces - 2), pieces)]
    merge(turns, rest[:-1], pieces)
    run(rest[-1:])
    keep(2, tokens_t, token_rows)
    run(ends0[:pieces - held_back])
    gathered(1)
    stored[3].start()
    turns = [call(compute, 1, 0)]
    for p in range(1, pieces):
        turns += [call(compute, 1, p), call(reduce_pair, 1, p - 1)]
    merge(turns + [call(reduce_pair, 1, pieces - 1)], ends0[pieces - held_back:], 3)
    arrive(0)
    merge(outs0, ends1[:pieces - held_back], 0)
    keep(0, act_t, act)
    early = max(1, chunks - 2)
    merge(nears0[:early], ends1[pieces - held_back:], 0)
    arrive(1)
    stored[1].start()
    merge(outs1, nears0[early:], 1)
    merge(nears1, each(settle, 0, chunks), 0)
    run(each(settle, 1, chunks))
    for copy in stored:
        copy.wait()
    for copy in sent:
        copy.wait_send()


ANY = pl.BlockSpec(memory_space=pl.ANY)


def layer_stage(far, near, chips, cores, first, second, masks, down, up):
    depth, width = down.shape
    tokens = first.shape[0] * far * near
    cols, span = cut(width, COLS), cut(depth, SPAN)
    pieces, chunks = width // cols, depth // span
    half, share = tokens // cores, tokens // (far * near)
    full = (far * near,) + first.shape
    bf16, f32 = jnp.bfloat16, jnp.float32
    tokens_t, act_t, hid, grad_rows, mixed, tokens_grad = pl.pallas_call(
        functools.partial(layer_kernel, far, near, chips, cores),
        out_shape=(
            jax.ShapeDtypeStruct((depth, tokens), bf16), jax.ShapeDtypeStruct((width, tokens), bf16),
            jax.ShapeDtypeStruct((cores, half, width), bf16), jax.ShapeDtypeStruct(full, bf16),
            jax.ShapeDtypeStruct((share, depth), bf16), jax.ShapeDtypeStruct((share, depth), bf16),
        ),
        in_specs=[ANY] * 6,
        out_specs=(ANY,) * 4 + (VMEM,) * 2,
        scratch_shapes=[
            pltpu.VMEM((depth // BLK * SUB, width), bf16), pltpu.VMEM((width // BLK * SUB, depth), bf16),
            pltpu.VMEM((depth, width), bf16), pltpu.VMEM((width, depth), bf16), DMA((pieces,)), DMA((pieces,)),
            pltpu.VMEM(full, bf16), pltpu.VMEM((cores, half, width), bf16),
            DMA((2, far - 1)), DMA((2, far - 1)), DMA((2, far, near - 1)), DMA((2, far, near - 1)), DMA((2,)),
            pltpu.VMEM((2, pieces, cores, half, cols), f32), pltpu.VMEM((2, pieces, half, cols), f32),
            pltpu.VMEM((2, pieces, half, cols), bf16), pltpu.VMEM((2, pieces, chips - 1, half, cols), bf16),
            pltpu.VMEM((pieces, half, cols), f32),
            DMA((2, pieces)), DMA((2, pieces)),
            DMA((2, pieces, chips - 1)), DMA((2, pieces, chips - 1)),
            DMA((2, pieces)), DMA((2, pieces)),
            pltpu.VMEM((2, chunks, far, near, share, span), f32),
            pltpu.VMEM((2, chunks, far, near, share, span), bf16),
            pltpu.VMEM((2, chunks, near - 1, far, share, span), bf16),
            pltpu.VMEM((2, chunks, far - 1, share, span), bf16),
            pltpu.VMEM((2, chunks, far - 1, share, span), bf16),
            DMA((2, chunks, near - 1)), DMA((2, chunks, near - 1)),
            DMA((2, chunks, far - 1)), DMA((2, chunks, far - 1)),
            pltpu.VMEM((depth, tokens), bf16), pltpu.VMEM((width, tokens), bf16),
            pltpu.VMEM((cores, half, width), bf16), pltpu.VMEM(full, bf16),
            pltpu.VMEM(masks[0].shape, masks[0].dtype), pltpu.VMEM(masks[1].shape, masks[1].dtype),
            DMA((2,)), DMA((4,)),
        ],
        compiler_params=pltpu.CompilerParams(
            collective_id=0, has_side_effects=True, vmem_limit_bytes=67043328
        ),
        name="layer_stage",
    )(first, second, *masks, down, up)
    flat = lambda each: each.reshape(tokens, each.shape[-1])
    return tokens_t, act_t, flat(hid), flat(grad_rows), mixed, tokens_grad


def outer_kernel(tokens_ref, hid_ref, in_mask, act_ref, grad_ref, out_mask, mixed_ref, back_ref, *outs):
    in_ref, out_ref, mixed_out, back_out = outs
    step = pl.program_id(0)

    @pl.when(step == 0)
    def _():
        mixed_out[...] = mixed_ref[...]
        back_out[...] = back_ref[...]

    def one(left, right, mask, out):
        down, across = out.shape[0] // BLK, out.shape[1] // BLK
        full = jnp.dot(left[...], right[...], preferred_element_type=jnp.float32)
        for b in range(down):
            for c in range(across):
                block = slice(b * BLK, (b + 1) * BLK), slice(c * BLK, (c + 1) * BLK)
                out[block] = (full[block] * mask[step * down + b, c].astype(jnp.float32)).astype(out.dtype)

    one(tokens_ref, hid_ref, in_mask, in_ref)
    one(act_ref, grad_ref, out_mask, out_ref)


def outers(tokens, hid, in_mask, act, grad, out_mask, mixed, back):
    depth, count = tokens.shape
    width = hid.shape[1]
    steps = math.gcd(depth // BLK, width // BLK)
    while steps % 2 == 0 and depth // steps < STEP:
        steps //= 2
    down, up = depth // steps, width // steps
    whole = lambda each: pl.BlockSpec(each.shape, lambda i: (0, 0))
    same = lambda each: jax.ShapeDtypeStruct(each.shape, each.dtype)
    return pl.pallas_call(
        outer_kernel,
        grid=(steps,),
        out_shape=[
            jax.ShapeDtypeStruct((depth, width), jnp.bfloat16), jax.ShapeDtypeStruct((width, depth), jnp.bfloat16),
            same(mixed), same(back),
        ],
        in_specs=[
            pl.BlockSpec((down, count), lambda i: (i, 0)), whole(hid), SMEM,
            pl.BlockSpec((up, count), lambda i: (i, 0)), whole(grad), SMEM,
            whole(mixed), whole(back),
        ],
        out_specs=[
            pl.BlockSpec((down, width), lambda i: (i, 0)), pl.BlockSpec((up, depth), lambda i: (i, 0)),
            whole(mixed), whole(back),
        ],
        name="outers",
    )(tokens, hid, in_mask, act, grad, out_mask, mixed, back)


def local(far, near, chips, cores, tokens, w_in, w_out, mask_in, mask_out, out_grad):
    tokens_t, act_t, hid, grad_rows, mixed, tokens_grad = layer_stage(
        far, near, chips, cores, tokens, out_grad, (mask_in, mask_out), w_in, w_out
    )
    w_in_grad, w_out_grad, mixed, tokens_grad = outers(
        tokens_t, hid, mask_in, act_t, grad_rows, mask_out, mixed, tokens_grad
    )
    return (mixed, tokens_grad, w_in_grad, w_out_grad)


def solution(mesh):
    columns, rows = mesh.shape["col"], mesh.shape["row"]
    near = 2 ** (int(math.log2(columns)) // 2)
    return jax.shard_map(
        functools.partial(local, columns // near, near, rows // 2, 2),
        mesh=mesh,
        in_specs=(
            P("col", "row"),
            P("row", "col"),
            P("col", "row"),
            P("row", "col"),
            P("col", "row"),
            P("col", "row"),
        ),
        out_specs=(P("col", "row"), P("col", "row"), P("row", "col"), P("col", "row")),
        check_vma=False,
    )
```
